32 devices in a mesh: bx: 4 (over z), by: 8 (over y, x, core).
Axes of the slice: x: 2, y: 2, z: 4, core: 2. Of those that a mesh axis runs over, the one named last changes fastest.
Arguments:
- fixed_image: bfloat16 [256, 512, 128], P('bx', 'by'), may hold values from -6 to 6
- moving_image: bfloat16 [256, 512, 128], P('bx', 'by'), may hold values from -6 to 6
- source_list: int32 [4, 8, 8], P('bx'), may hold values from 0 to 7, each once within a row
- stretch_offsets: int32 [4, 8, 2], P('bx', 'by'), may hold values from -4 to 4
Outputs:
- displacement: float32 [3, 256, 512, 128], P(None, 'bx', 'by')
- back_force: float32 [3, 256, 512, 128], P(None, 'bx', 'by')
The draws below stay inside these ranges and needn't reach their ends.
Inputs may be any that keep to these rules, and one draw needn't show every extreme that they name: `source_list`: for each brick, its entries name every column of bricks exactly once.
All inputs are finite; a program needn't handle non-finite values.
Results may differ from the reference program's by a relative error of at most 0.004.
Values may be sent and summed in bfloat16 or wider, within the bound.
A program may use at most 320 MiB of HBM per device.

```python
import jax
import jax.numpy as jnp
from jax import lax

BY = 64
BZ = 128
RADIUS = 8
ITERS = 3
NX = 256
NY = 512
XS = 8
N_BX = 4
N_BY = 8


def touch_ends(drawn, rng, least, high):
    shape = drawn.shape
    spot = [jax.random.randint(jax.random.fold_in(rng, axis), (), 0, shape[axis]) for axis in range(len(shape))]
    drawn = drawn.at[tuple(spot)].set(least)
    longest = shape.index(max(shape))
    spot[longest] = (spot[longest] + 1) % shape[longest]
    return drawn.at[tuple(spot)].set(high)


def block_levels(key, shape, shards, low, high):
    def one(axis_at, blocks):
        draws = jax.random.uniform(jax.random.fold_in(jax.random.fold_in(key, 6), axis_at), (blocks,), jnp.float32, low / len(shards), high / len(shards))
        return jnp.repeat(jnp.exp(draws), shape[axis_at] // blocks).reshape((-1,) + (1,) * (len(shape) - axis_at - 1))

    gain = one(*shards[0])
    for cut in shards[1:]:
        gain = gain * one(*cut)
    return gain


def normal_values(own_key, shape, scale, most, split=(), kind=jnp.bfloat16):
    factor_of = block_levels(own_key, shape, split, -0.22, 0.18) if split else 1.0
    entries = jax.random.normal(own_key, shape, jnp.float32) * scale * factor_of
    return jnp.minimum(jnp.maximum(entries, -most), most).astype(kind)


def setup_inputs(seed: int = 0) -> dict:
    splits = jax.random.split(jax.random.key(seed), 5)
    fixed_image = normal_values(splits[0], (NX, NY, BZ), 1.0, 6.0, ((0, 4), (1, 8)))
    moving_image = normal_values(splits[1], (NX, NY, BZ), 1.0, 6.0, ((0, 4), (1, 8)))
    source_list = jax.vmap(lambda own: jax.random.permutation(own, N_BY))(jax.random.split(splits[2], N_BX * N_BY)).reshape((N_BX, N_BY, N_BY)).astype(jnp.int32)
    stretch_offsets = touch_ends(jax.random.randint(splits[3], (N_BX, N_BY, 2), -4, 5), jax.random.fold_in(splits[3], 1), -4, 4).astype(jnp.int32)
    return dict(fixed_image=fixed_image, moving_image=moving_image, source_list=source_list, stretch_offsets=stretch_offsets)


STEP_SIZE = 128.0


def stretch_matrix(length, offset):
    index = jnp.arange(length).astype(jnp.float32)
    place = index + offset.astype(jnp.float32) * (2.0 * index + 1.0 - length) / (2.0 * length)
    place = jnp.clip(place, 0.0, length - 1.0)
    return jnp.maximum(0.0, 1.0 - jnp.abs(place[:, None] - index[None, :]))


def gauss_weights():
    spread = 0.75 * RADIUS
    offs = jnp.arange(-RADIUS, RADIUS + 1).astype(jnp.float32)
    raw = jnp.exp(-offs * offs / (2.0 * spread * spread))
    return raw / jnp.sum(raw)


def smooth_axis(field, axis, weights):
    widths = [(0, 0)] * field.ndim
    widths[axis] = (RADIUS, RADIUS)
    padded = jnp.pad(field, widths)
    count = field.shape[axis]
    total = jnp.zeros(field.shape, jnp.float32)
    for j in range(2 * RADIUS + 1):
        total = total + weights[j] * lax.slice_in_dim(padded, j, j + count, axis=axis)
    return total


def smooth_field(field):
    weights = gauss_weights()

    def one(comp):
        out = smooth_axis(comp, 0, weights)
        out = smooth_axis(out, 1, weights)
        return smooth_axis(out, 2, weights)

    return lax.map(one, field)


def central(field):
    padded = jnp.pad(field, 1)
    grad_x = (padded[2:, 1:-1, 1:-1] - padded[:-2, 1:-1, 1:-1]) * 0.5
    grad_y = (padded[1:-1, 2:, 1:-1] - padded[1:-1, :-2, 1:-1]) * 0.5
    grad_z = (padded[1:-1, 1:-1, 2:] - padded[1:-1, 1:-1, :-2]) * 0.5
    return jnp.stack([grad_x, grad_y, grad_z])


def pushed(field_u, warped_f, fixed_f, grad_moving, grad_mean):
    moved = warped_f + jnp.sum(field_u * grad_moving, axis=0)
    differ = moved - fixed_f
    denom = jnp.sum(grad_mean * grad_mean, axis=0) + differ * differ + 1.0
    return field_u + STEP_SIZE * (differ / denom)[None] * grad_mean


def reference(fixed_image, moving_image, source_list, stretch_offsets):
    hi = lax.Precision.HIGHEST
    bricks = moving_image.reshape(N_BX, N_BY, XS, N_BY, BY, BZ).transpose(0, 3, 1, 2, 4, 5)
    row_idx = jnp.arange(N_BX).astype(jnp.int32)[:, None, None]
    slab_idx = jnp.arange(N_BY).astype(jnp.int32)[None, None, :]
    pieces = bricks[row_idx, source_list.astype(jnp.int32), slab_idx]
    flat_off = stretch_offsets.reshape(N_BX * N_BY, 2)
    stretch_y = jax.vmap(lambda o: stretch_matrix(BY, o))(flat_off[:, 0]).reshape(N_BX, N_BY, BY, BY)
    stretch_z = jax.vmap(lambda o: stretch_matrix(BZ, o))(flat_off[:, 1]).reshape(N_BX, N_BY, BZ, BZ)
    first = jnp.einsum("abyc,abkxcz->abkxyz", stretch_y, pieces.astype(jnp.float32), precision=hi)
    second = jnp.einsum("abkxyz,abwz->abkxyw", first, stretch_z, precision=hi)
    warped = second.astype(jnp.bfloat16).transpose(0, 2, 3, 1, 4, 5).reshape(NX, NY, BZ)
    warped_f = warped.astype(jnp.float32)
    fixed_f = fixed_image.astype(jnp.float32)
    grad_moving = central(warped_f)
    grad_mean = 0.5 * (central(fixed_f) + grad_moving)
    field_u = jnp.zeros((3, NX, NY, BZ), jnp.float32)
    for step in range(ITERS):
        field_v = pushed(field_u, warped_f, fixed_f, grad_moving, grad_mean)
        field_u = smooth_field(field_v)
    parts = field_u.reshape(3, N_BX, N_BY, XS, N_BY, BY, BZ).transpose(1, 4, 2, 0, 3, 5, 6)
    turned = jnp.einsum("abkcxyz,abyv->abkcxvz", parts, stretch_y, precision=hi)
    turned = jnp.einsum("abkcxvz,abzw->abkcxvw", turned, stretch_z, precision=hi)
    turned = turned.astype(jnp.bfloat16).astype(jnp.float32)
    chosen = (source_list[..., None] == jnp.arange(N_BY).astype(jnp.int32)[None, None, None, :]).astype(jnp.float32)
    back = jnp.einsum("abks,abkcxyz->askcxyz", chosen, turned, precision=hi)
    back_force = back.transpose(3, 0, 2, 4, 1, 5, 6).reshape(3, NX, NY, BZ)
    return field_u, back_force
```

```python
import jax
import jax.numpy as jnp
import ml_dtypes
import numpy as np
from jax import lax
from jax.sharding import PartitionSpec as P

RADIUS = 8
ITERS = 3


STEP_SIZE = 128.0


def padded_2(x, sides, width):
    for axis, dim in sides:
        peers, length = (lax.axis_size(axis), x.shape[dim])
        up = [(i, (i + 1) % peers) for i in range(peers - 1)]
        down = [(j, i) for i, j in up]
        last = lax.slice_in_dim(x, length - width, length, axis=dim)
        initial = lax.slice_in_dim(x, 0, width, axis=dim)
        before = lax.ppermute(last, axis, up)
        after = lax.ppermute(initial, axis, down)
        x = jnp.concatenate([before, x, after], axis=dim)
    return x


def stretch_matrix(length, offset):
    index = jnp.arange(length).astype(jnp.float32)
    place = index + offset.astype(jnp.float32) * (2.0 * index + 1.0 - length) / (2.0 * length)
    place = jnp.clip(place, 0.0, length - 1.0)
    return jnp.maximum(0.0, 1.0 - jnp.abs(place[:, None] - index[None, :]))


def tap_weights():
    spread = 0.75 * RADIUS
    offs = np.arange(-RADIUS, RADIUS + 1).astype(np.float64)
    raw = np.exp(-offs * offs / (2.0 * spread * spread))
    raw = raw / raw.sum()
    best = None
    for scale in np.linspace(4.0, 8.0, 2001):
        near = (raw * scale).astype(ml_dtypes.bfloat16).astype(np.float64)
        err = np.sum((near / near.sum() - raw) ** 2)
        if best is None or err < best[0]:
            best = (err, near)
    near = best[1]
    return near, 1.0 / near.sum()


TAPS, UNSCALE = tap_weights()


def band(rows, cols):
    start = (cols - rows) // 2
    dist = np.arange(cols)[None, :] - np.arange(rows)[:, None] - start
    inside = np.abs(dist) <= RADIUS
    return jnp.asarray(np.where(inside, TAPS[np.clip(dist + RADIUS, 0, 2 * RADIUS)], 0.0).astype(ml_dtypes.bfloat16))


def dot(spec, a, b):
    return jnp.einsum(spec, a, b, preferred_element_type=jnp.float32)


def halves(x):
    high = lax.reduce_precision(x, 8, 7)
    return high.astype(jnp.bfloat16), (x - high).astype(jnp.bfloat16)


def dot_split(spec, x, w):
    high, low = halves(x)
    return dot(spec, high, w) + dot(spec, low, w)


def smooth(field):
    rows, cols, depth = field.shape[1:]
    first = dot_split("cabz,wz->cabw", field, band(depth, depth)) * UNSCALE
    grown = padded_2(first.astype(jnp.bfloat16), (("bx", 1),), RADIUS)
    second = dot("ia,cabz->cibz", band(rows, rows + 2 * RADIUS), grown) * UNSCALE
    grown = padded_2(second.astype(jnp.bfloat16), (("by", 2),), RADIUS)
    return dot("jb,cibz->cijz", band(cols, cols + 2 * RADIUS), grown) * UNSCALE


def central(padded):
    zpad = jnp.pad(padded, ((0, 0), (0, 0), (1, 1)))
    grad_x = (zpad[2:, 1:-1, 1:-1] - zpad[:-2, 1:-1, 1:-1]) * 0.5
    grad_y = (zpad[1:-1, 2:, 1:-1] - zpad[1:-1, :-2, 1:-1]) * 0.5
    grad_z = (zpad[1:-1, 1:-1, 2:] - zpad[1:-1, 1:-1, :-2]) * 0.5
    return jnp.stack([grad_x, grad_y, grad_z])


def pushed(field_u, warped_f, fixed_f, grad_moving, grad_mean):
    moved = warped_f + jnp.sum(field_u * grad_moving, axis=0)
    differ = moved - fixed_f
    denom = jnp.sum(grad_mean * grad_mean, axis=0) + differ * differ + 1.0
    return field_u + STEP_SIZE * (differ / denom)[None] * grad_mean


def local(fixed_image, moving_image, source_list, stretch_offsets):
    width_x, width_y, depth = fixed_image.shape
    peers = lax.axis_size("by")
    mine = lax.axis_index("by")
    rows_slab = width_x // peers
    lists = source_list[0]
    own_list = lax.dynamic_index_in_dim(lists, mine, 0, keepdims=False)
    slab_ids = jnp.arange(peers)
    asked = (lists == mine).astype(jnp.int32)
    wanted = jnp.sum(asked * slab_ids[None, :], axis=1)
    slabs = moving_image.reshape(peers, rows_slab, width_y, depth)
    outgoing = jnp.take(slabs, wanted, axis=0)
    incoming = lax.all_to_all(outgoing, "by", split_axis=0, concat_axis=0, tiled=True)
    offsets = stretch_offsets[0, 0]
    stretch_y = stretch_matrix(width_y, offsets[0])
    stretch_z = stretch_matrix(depth, offsets[1])
    first = jnp.einsum(
        "yc,pxcz->pxyz",
        stretch_y.astype(jnp.bfloat16),
        incoming,
        preferred_element_type=jnp.float32,
    )
    second = dot_split("pxyz,wz->pxyw", first, stretch_z.astype(jnp.bfloat16))
    stretched = second.astype(jnp.bfloat16)
    warped = jnp.take(stretched, own_list, axis=0).reshape(width_x, width_y, depth)
    stacked = jnp.stack([fixed_image, warped])
    grown = padded_2(stacked, (("bx", 1), ("by", 2)), 1)
    grad_moving = central(grown[1].astype(jnp.float32))
    grad_mean = 0.5 * (central(grown[0].astype(jnp.float32)) + grad_moving)
    fixed_f = fixed_image.astype(jnp.float32)
    warped_f = warped.astype(jnp.float32)
    field_u = jnp.zeros((3, width_x, width_y, depth), jnp.float32)
    for step in range(ITERS):
        field_v = pushed(field_u, warped_f, fixed_f, grad_moving, grad_mean)
        field_u = smooth(field_v)
    pieces_u = field_u.reshape(3, peers, rows_slab, width_y, depth)
    turned = dot_split("ckxyz,yv->ckxvz", pieces_u, stretch_y.astype(jnp.bfloat16))
    turned = dot_split("ckxvz,zw->ckxvw", turned, stretch_z.astype(jnp.bfloat16)).astype(jnp.bfloat16)
    inverse = jnp.sum(
        (own_list[None, :] == slab_ids[:, None]).astype(jnp.int32) * slab_ids[None, :], axis=1
    )
    sending = jnp.take(turned, inverse, axis=1)
    arriving = lax.all_to_all(sending, "by", split_axis=1, concat_axis=1, tiled=True)
    table = asked.astype(jnp.bfloat16)
    back = jnp.einsum("tk,ctxyz->ckxyz", table, arriving, preferred_element_type=jnp.float32)
    back_force = back.reshape(3, width_x, width_y, depth)
    return (field_u, back_force)


def solution(mesh):
    return jax.shard_map(
        local,
        mesh=mesh,
        in_specs=(
            P("bx", "by", None),
            P("bx", "by", None),
            P("bx", None, None),
            P("bx", "by", None),
        ),
        out_specs=(P(None, "bx", "by", None), P(None, "bx", "by", None)),
        check_vma=False,
    )
```

```python
import functools

import jax
import jax.numpy as jnp
import ml_dtypes
import numpy as np
from jax import lax
from jax.experimental import pallas as pl
from jax.experimental.pallas import tpu as pltpu
from jax.sharding import PartitionSpec as P

RADIUS = 8
ITERS = 3


STEP_SIZE = 128.0


def padded_2(x, sides, width):
    for axis, dim in sides:
        peers, length = (lax.axis_size(axis), x.shape[dim])
        up = [(i, (i + 1) % peers) for i in range(peers - 1)]
        down = [(j, i) for i, j in up]
        last = lax.slice_in_dim(x, length - width, length, axis=dim)
        initial = lax.slice_in_dim(x, 0, width, axis=dim)
        before = lax.ppermute(last, axis, up)
        after = lax.ppermute(initial, axis, down)
        x = jnp.concatenate([before, x, after], axis=dim)
    return x


def stretch_matrix(length, offset):
    index = jnp.arange(length).astype(jnp.float32)
    place = index + offset.astype(jnp.float32) * (2.0 * index + 1.0 - length) / (2.0 * length)
    place = jnp.clip(place, 0.0, length - 1.0)
    return jnp.maximum(0.0, 1.0 - jnp.abs(place[:, None] - index[None, :]))


def tap_weights():
    spread = 0.75 * RADIUS
    offs = np.arange(-RADIUS, RADIUS + 1).astype(np.float64)
    raw = np.exp(-offs * offs / (2.0 * spread * spread))
    raw = raw / raw.sum()
    best = None
    for scale in np.linspace(4.0, 8.0, 2001):
        near = (raw * scale).astype(ml_dtypes.bfloat16).astype(np.float64)
        err = np.sum((near / near.sum() - raw) ** 2)
        if best is None or err < best[0]:
            best = (err, near)
    near = best[1]
    return raw, near, 1.0 / near.sum()


EXACT, TAPS, UNSCALE = tap_weights()
UNSCALE = float(UNSCALE)


def band(rows, cols):
    start = (cols - rows) // 2
    dist = np.arange(cols)[None, :] - np.arange(rows)[:, None] - start
    inside = np.abs(dist) <= RADIUS
    return jnp.asarray(np.where(inside, TAPS[np.clip(dist + RADIUS, 0, 2 * RADIUS)], 0.0).astype(ml_dtypes.bfloat16))


def dot(spec, a, b):
    return jnp.einsum(spec, a, b, preferred_element_type=jnp.float32)


def halves(x):
    high = lax.reduce_precision(x, 8, 7)
    return high.astype(jnp.bfloat16), (x - high).astype(jnp.bfloat16)


def dot_split(spec, x, w):
    high, low = halves(x)
    return dot(spec, high, w) + dot(spec, low, w)


def demons_kernel(nx, ny, d0_ref, gm_ref, gn_ref, wy_ref, wz_ref, u_ref, zs, xs, xsend, xrecv, ysend, yrecv, xss, xrs, yss, yrs):
    comps, width_x, width_y, depth = gm_ref.shape
    ix, iy = lax.axis_index("bx"), lax.axis_index("by")
    has = {"bx": (ix > 0, ix < nx - 1), "by": (iy > 0, iy < ny - 1)}
    dev = {
        "bx": (lax.rem(ix + nx - 1, nx), lax.rem(ix + 1, nx)),
        "by": (lax.rem(iy + ny - 1, ny), lax.rem(iy + 1, ny)),
    }
    barrier = pltpu.get_barrier_semaphore()
    for axis in ("bx", "by"):
        for side in (0, 1):

            @pl.when(has[axis][side])
            def _():
                pl.semaphore_signal(barrier, inc=1, device_id={axis: dev[axis][side]}, device_id_type=pl.DeviceIdType.MESH)

    met = sum(ok.astype(jnp.int32) for axis in ("bx", "by") for ok in has[axis])
    pl.semaphore_wait(barrier, met)

    def copy(axis, it, side, c):
        send, recv, ss, rs = (xsend, xrecv, xss, xrs) if axis == "bx" else (ysend, yrecv, yss, yrs)
        return pltpu.make_async_remote_copy(
            src_ref=send.at[it, side, c],
            dst_ref=recv.at[it, 1 - side, c],
            send_sem=ss.at[it, side, c],
            recv_sem=rs.at[it, 1 - side, c],
            device_id={axis: dev[axis][side]},
            device_id_type=pl.DeviceIdType.MESH,
        )

    def start(axis, it, side, c):
        @pl.when(has[axis][side])
        def _():
            copy(axis, it, side, c).start()

    R = RADIUS
    for side in (0, 1):
        at_x = 0 if side == 0 else R + width_x
        at_y = 0 if side == 0 else R + width_y

        @pl.when(jnp.logical_not(has["bx"][side]))
        def _():
            for c in range(comps):
                zs[c, at_x : at_x + R] = jnp.zeros((R, width_y, depth), jnp.float32)

        @pl.when(jnp.logical_not(has["by"][side]))
        def _():
            for c in range(comps):
                xs[c, :, at_y : at_y + R, :] = jnp.zeros((width_x, R, depth), jnp.float32)

    def field_pair(x):
        rhs = jnp.concatenate([xs[c, x + r] for c in range(comps) for r in range(2)], axis=1).astype(jnp.bfloat16)
        out = jnp.dot(wy_ref[...], rhs, preferred_element_type=jnp.float32) * UNSCALE
        return [[out[:, (2 * c + r) * depth : (2 * c + r + 1) * depth] for c in range(comps)] for r in range(2)]

    def force_pair(x, it):
        field = field_pair(x) if it else None
        parts = [None] * (2 * comps)
        for r in range(2):
            differ = d0_ref[x + r]
            grads = [gn_ref[c, x + r] for c in range(comps)]
            denom = 1.0
            for c in range(comps):
                denom = denom + grads[c] * grads[c]
                if it:
                    differ = differ + field[r][c] * gm_ref[c, x + r]
            gain = STEP_SIZE * (differ / (denom + differ * differ))
            for c in range(comps):
                pushed_c = gain * grads[c]
                if it:
                    pushed_c = pushed_c + field[r][c]
                high = pushed_c.astype(jnp.bfloat16)
                low = (pushed_c - high.astype(jnp.float32)).astype(jnp.bfloat16)
                parts[2 * c + r] = jnp.concatenate([high, low], axis=1)
        lhs = jnp.concatenate(parts, axis=0)
        out = jnp.dot(lhs, wz_ref[...], preferred_element_type=jnp.float32) * UNSCALE
        for c in range(comps):
            for r in range(2):
                at = (2 * c + r) * width_y
                zs[c, R + x + r] = out[at : at + width_y]

    half = R // 2
    pairs = width_x // 2
    blocks_x, blocks_y = width_x // R, width_y // R
    for it in range(ITERS):

        @pl.loop(0, 2 * half)
        def _(p):
            force_pair(2 * (p + (p // half) * (pairs - 2 * half)), it)

        for c in range(comps):
            for side in (0, 1):
                at = R if side == 0 else width_x
                xsend[it, side, c] = zs[c, at : at + R].astype(jnp.bfloat16)
                start("bx", it, side, c)

        @pl.loop(half, pairs - half)
        def _(p):
            force_pair(2 * p, it)

        for c in range(comps):
            for side in (0, 1):
                at = 0 if side == 0 else R + width_x

                @pl.when(has["bx"][side])
                def _():
                    copy("bx", it, 1 - side, c).wait_recv()
                    zs[c, at : at + R] = xrecv[it, side, c].astype(jnp.float32)

            @pl.loop(0, blocks_x * blocks_y)
            def _(t):
                x0 = (t // blocks_y) * R
                y0 = pl.multiple_of((t % blocks_y) * R, R)
                block = zs[c, pl.ds(x0, 3 * R), pl.ds(y0, R), :]
                total = block[R : 2 * R] * float(EXACT[R])
                for d in range(1, R + 1):
                    total = total + (block[R - d : 2 * R - d] + block[R + d : 2 * R + d]) * float(EXACT[R + d])
                xs[c, pl.ds(x0, R), pl.ds(pl.multiple_of(y0 + R, R), R), :] = total

            @pl.loop(0, blocks_x)
            def _(t):
                for side in (0, 1):
                    at = R if side == 0 else width_y
                    edge = xs[c, pl.ds(t * R, R), at : at + R, :]
                    ysend[it, side, c, pl.ds(t * half, half)] = edge.reshape(half, 2 * R, depth).astype(jnp.bfloat16)

            for side in (0, 1):
                start("by", it, side, c)

        for c in range(comps):
            for side in (0, 1):
                at = 0 if side == 0 else R + width_y

                @pl.when(has["by"][side])
                def _():
                    copy("by", it, 1 - side, c).wait_recv()

                    @pl.loop(0, blocks_x)
                    def _(t):
                        got = yrecv[it, side, c, pl.ds(t * half, half)].astype(jnp.float32)
                        xs[c, pl.ds(t * R, R), at : at + R, :] = got.reshape(R, R, depth)

    @pl.loop(0, pairs)
    def _(p):
        field = field_pair(2 * p)
        for r in range(2):
            for c in range(comps):
                u_ref[c, 2 * p + r] = field[r][c]

    for it in range(ITERS):
        for axis in ("bx", "by"):
            for side in (0, 1):
                for c in range(comps):

                    @pl.when(has[axis][side])
                    def _():
                        copy(axis, it, side, c).wait_send()


def demons(d0, gm, gn):
    comps, width_x, width_y, depth = gm.shape
    grid_x, grid_y = lax.axis_size("bx"), lax.axis_size("by")
    wz = band(depth, depth)
    vmem = pl.BlockSpec(memory_space=pltpu.VMEM)
    edge_x = pltpu.VMEM((ITERS, 2, comps, RADIUS, width_y, depth), jnp.bfloat16)
    edge_y = pltpu.VMEM((ITERS, 2, comps, width_x // 2, 2 * RADIUS, depth), jnp.bfloat16)
    sems = pltpu.SemaphoreType.DMA((ITERS, 2, comps))
    return pl.pallas_call(
        functools.partial(demons_kernel, grid_x, grid_y),
        out_shape=jax.ShapeDtypeStruct(gm.shape, jnp.float32),
        in_specs=[vmem] * 5,
        out_specs=vmem,
        scratch_shapes=[
            pltpu.VMEM((comps, width_x + 2 * RADIUS, width_y, depth), jnp.float32),
            pltpu.VMEM((comps, width_x, width_y + 2 * RADIUS, depth), jnp.float32),
            edge_x,
            edge_x,
            edge_y,
            edge_y,
            sems,
            sems,
            sems,
            sems,
        ],
        compiler_params=pltpu.CompilerParams(collective_id=0, has_side_effects=True, vmem_limit_bytes=60 << 20),
    )(d0, gm, gn, band(width_y, width_y + 2 * RADIUS), jnp.concatenate([wz, wz], axis=0))


def central(padded):
    zpad = jnp.pad(padded, ((0, 0), (0, 0), (1, 1)))
    grad_x = (zpad[2:, 1:-1, 1:-1] - zpad[:-2, 1:-1, 1:-1]) * 0.5
    grad_y = (zpad[1:-1, 2:, 1:-1] - zpad[1:-1, :-2, 1:-1]) * 0.5
    grad_z = (zpad[1:-1, 1:-1, 2:] - zpad[1:-1, 1:-1, :-2]) * 0.5
    return jnp.stack([grad_x, grad_y, grad_z])


def local(fixed_image, moving_image, source_list, stretch_offsets):
    width_x, width_y, depth = fixed_image.shape
    peers = lax.axis_size("by")
    mine = lax.axis_index("by")
    rows_slab = width_x // peers
    lists = source_list[0]
    own_list = lax.dynamic_index_in_dim(lists, mine, 0, keepdims=False)
    slab_ids = jnp.arange(peers)
    asked = (lists == mine).astype(jnp.int32)
    wanted = jnp.sum(asked * slab_ids[None, :], axis=1)
    slabs = moving_image.reshape(peers, rows_slab, width_y, depth)
    outgoing = jnp.take(slabs, wanted, axis=0)
    incoming = lax.all_to_all(outgoing, "by", split_axis=0, concat_axis=0, tiled=True)
    offsets = stretch_offsets[0, 0]
    stretch_y = stretch_matrix(width_y, offsets[0])
    stretch_z = stretch_matrix(depth, offsets[1])
    first = jnp.einsum(
        "yc,pxcz->pxyz",
        stretch_y.astype(jnp.bfloat16),
        incoming,
        preferred_element_type=jnp.float32,
    )
    second = dot_split("pxyz,wz->pxyw", first, stretch_z.astype(jnp.bfloat16))
    stretched = second.astype(jnp.bfloat16)
    warped = jnp.take(stretched, own_list, axis=0).reshape(width_x, width_y, depth)
    stacked = jnp.stack([fixed_image, warped])
    grown = padded_2(stacked, (("bx", 1), ("by", 2)), 1)
    grad_moving = central(grown[1].astype(jnp.float32))
    grad_mean = 0.5 * (central(grown[0].astype(jnp.float32)) + grad_moving)
    fixed_f = fixed_image.astype(jnp.float32)
    warped_f = warped.astype(jnp.float32)
    field_u = demons(warped_f - fixed_f, grad_moving, grad_mean)
    pieces_u = field_u.reshape(3, peers, rows_slab, width_y, depth)
    turned = dot_split("ckxyz,yv->ckxvz", pieces_u, stretch_y.astype(jnp.bfloat16))
    turned = dot_split("ckxvz,zw->ckxvw", turned, stretch_z.astype(jnp.bfloat16)).astype(jnp.bfloat16)
    inverse = jnp.sum(
        (own_list[None, :] == slab_ids[:, None]).astype(jnp.int32) * slab_ids[None, :], axis=1
    )
    sending = jnp.take(turned, inverse, axis=1)
    arriving = lax.all_to_all(sending, "by", split_axis=1, concat_axis=1, tiled=True)
    table = asked.astype(jnp.bfloat16)
    back = jnp.einsum("tk,ctxyz->ckxyz", table, arriving, preferred_element_type=jnp.float32)
    back_force = back.reshape(3, width_x, width_y, depth)
    return (field_u, back_force)


def solution(mesh):
    return jax.shard_map(
        local,
        mesh=mesh,
        in_specs=(
            P("bx", "by", None),
            P("bx", "by", None),
            P("bx", None, None),
            P("bx", "by", None),
        ),
        out_specs=(P(None, "bx", "by", None), P(None, "bx", "by", None)),
        check_vma=False,
    )
```

```python
import functools

import jax
import jax.numpy as jnp
import ml_dtypes
import numpy as np
from jax import lax
from jax.experimental import pallas as pl
from jax.experimental.pallas import tpu as pltpu
from jax.sharding import PartitionSpec as P

RADIUS = 8
ITERS = 3


STEP_SIZE = 128.0


def stretch_matrix(length, offset):
    index = jnp.arange(length).astype(jnp.float32)
    place = index + offset.astype(jnp.float32) * (2.0 * index + 1.0 - length) / (2.0 * length)
    place = jnp.clip(place, 0.0, length - 1.0)
    return jnp.maximum(0.0, 1.0 - jnp.abs(place[:, None] - index[None, :]))


def tap_weights():
    spread = 0.75 * RADIUS
    offs = np.arange(-RADIUS, RADIUS + 1).astype(np.float64)
    raw = np.exp(-offs * offs / (2.0 * spread * spread))
    raw = raw / raw.sum()
    best = None
    for scale in np.linspace(4.0, 8.0, 2001):
        near = (raw * scale).astype(ml_dtypes.bfloat16).astype(np.float64)
        err = np.sum((near / near.sum() - raw) ** 2)
        if best is None or err < best[0]:
            best = (err, near)
    near = best[1]
    return raw, near, 1.0 / near.sum()


EXACT, TAPS, UNSCALE = tap_weights()
UNSCALE = float(UNSCALE)


def band(rows, cols):
    start = (cols - rows) // 2
    dist = np.arange(cols)[None, :] - np.arange(rows)[:, None] - start
    inside = np.abs(dist) <= RADIUS
    return jnp.asarray(np.where(inside, TAPS[np.clip(dist + RADIUS, 0, 2 * RADIUS)], 0.0).astype(ml_dtypes.bfloat16))


def dot(spec, a, b):
    return jnp.einsum(spec, a, b, preferred_element_type=jnp.float32)


def halves(x):
    high = lax.reduce_precision(x, 8, 7)
    return high.astype(jnp.bfloat16), (x - high).astype(jnp.bfloat16)


def dot_split(spec, x, w):
    high, low = halves(x)
    return dot(spec, high, w) + dot(spec, low, w)


def demons_kernel(nx, ny, order, fixed_ref, warped_ref, wy_ref, wz_ref, sy_ref, sz_ref, u_ref, back_ref, d0_ref, gm_ref, gn_ref, tsend, esx, erx, esy, ery, ess, ers, tss, trs, own_sem, zs, xs, xsend, xrecv, ysend, yrecv, xss, xrs, yss, yrs):
    comps, width_x, width_y, depth = gm_ref.shape
    ix, iy = lax.axis_index("bx"), lax.axis_index("by")
    has = {"bx": (ix > 0, ix < nx - 1), "by": (iy > 0, iy < ny - 1)}
    dev = {
        "bx": (lax.rem(ix + nx - 1, nx), lax.rem(ix + 1, nx)),
        "by": (lax.rem(iy + ny - 1, ny), lax.rem(iy + 1, ny)),
    }
    barrier = pltpu.get_barrier_semaphore()
    for side in (0, 1):

        @pl.when(has["bx"][side])
        def _():
            pl.semaphore_signal(barrier, inc=1, device_id={"bx": dev["bx"][side]}, device_id_type=pl.DeviceIdType.MESH)

    for j in range(1, ny):
        pl.semaphore_signal(barrier, inc=1, device_id={"by": lax.rem(iy + j, ny)}, device_id_type=pl.DeviceIdType.MESH)
    met = sum(ok.astype(jnp.int32) for ok in has["bx"]) + (ny - 1)
    pl.semaphore_wait(barrier, met)

    R = RADIUS

    def edge_copy(n, axis, side):
        send, recv = (esx, erx) if axis == "bx" else (esy, ery)
        return pltpu.make_async_remote_copy(
            src_ref=send.at[side],
            dst_ref=recv.at[1 - side],
            send_sem=ess.at[n, side],
            recv_sem=ers.at[n, 1 - side],
            device_id={axis: dev[axis][side]},
            device_id_type=pl.DeviceIdType.MESH,
        )

    images = (fixed_ref, warped_ref)
    for m in range(2):
        esx[0, m] = images[m][0]
        esx[1, m] = images[m][width_x - 1]

    @pl.loop(0, width_x)
    def _(x):
        for m in range(2):
            row = images[m][x].astype(jnp.float32)
            zs[m, R + x] = row
            esy[0, m, pl.ds(x, 1), :] = row[0:1]
            esy[1, m, pl.ds(x, 1), :] = row[width_y - 1 : width_y]

    for n, axis in enumerate(("bx", "by")):
        for side in (0, 1):

            @pl.when(has[axis][side])
            def _():
                edge_copy(n, axis, side).start()

    for side in (0, 1):
        at = R - 1 if side == 0 else R + width_x

        @pl.when(has["bx"][side])
        def _():
            edge_copy(0, "bx", 1 - side).wait_recv()
            for m in range(2):
                zs[m, at] = erx[side, m].astype(jnp.float32)

        @pl.when(jnp.logical_not(has["bx"][side]))
        def _():
            for m in range(2):
                zs[m, at] = jnp.zeros((width_y, depth), jnp.float32)

        @pl.when(has["by"][side])
        def _():
            edge_copy(1, "by", 1 - side).wait_recv()

        @pl.when(jnp.logical_not(has["by"][side]))
        def _():
            ery[side] = jnp.zeros(ery.shape[1:], jnp.float32)

    at_y = lax.broadcasted_iota(jnp.int32, (width_y, depth), 0)
    at_z = lax.broadcasted_iota(jnp.int32, (width_y, depth), 1)

    @pl.loop(0, width_x)
    def _(x):
        both = []
        for m in range(2):
            row = zs[m, R + x]
            grad_x = (zs[m, R + x + 1] - zs[m, R + x - 1]) * 0.5
            low = jnp.where(at_y == 0, ery[0, m, pl.ds(x, 1), :], pltpu.roll(row, 1, 0))
            high = jnp.where(at_y == width_y - 1, ery[1, m, pl.ds(x, 1), :], pltpu.roll(row, width_y - 1, 0))
            grad_y = (high - low) * 0.5
            low = jnp.where(at_z == 0, 0.0, pltpu.roll(row, 1, 1))
            high = jnp.where(at_z == depth - 1, 0.0, pltpu.roll(row, depth - 1, 1))
            both.append((grad_x, grad_y, (high - low) * 0.5))
        for c in range(comps):
            gm_ref[c, x] = both[1][c]
            gn_ref[c, x] = 0.5 * (both[0][c] + both[1][c])
        d0_ref[x] = zs[1, R + x] - zs[0, R + x]

    def copy(axis, it, side, c):
        send, recv, ss, rs = (xsend, xrecv, xss, xrs) if axis == "bx" else (ysend, yrecv, yss, yrs)
        return pltpu.make_async_remote_copy(
            src_ref=send.at[it, side, c],
            dst_ref=recv.at[it, 1 - side, c],
            send_sem=ss.at[it, side, c],
            recv_sem=rs.at[it, 1 - side, c],
            device_id={axis: dev[axis][side]},
            device_id_type=pl.DeviceIdType.MESH,
        )

    def start(axis, it, side, c):
        @pl.when(has[axis][side])
        def _():
            copy(axis, it, side, c).start()

    for side in (0, 1):
        at_x = 0 if side == 0 else R + width_x
        at_y = 0 if side == 0 else R + width_y

        @pl.when(jnp.logical_not(has["bx"][side]))
        def _():
            for c in range(comps):
                zs[c, at_x : at_x + R] = jnp.zeros((R, width_y, depth), jnp.float32)

        @pl.when(jnp.logical_not(has["by"][side]))
        def _():
            for c in range(comps):
                xs[c, :, at_y : at_y + R, :] = jnp.zeros((width_x, R, depth), jnp.float32)

    def field_pair(x):
        rhs = jnp.concatenate([xs[c, x + r] for c in range(comps) for r in range(2)], axis=1).astype(jnp.bfloat16)
        out = jnp.dot(wy_ref[...], rhs, preferred_element_type=jnp.float32) * UNSCALE
        return [[out[:, (2 * c + r) * depth : (2 * c + r + 1) * depth] for c in range(comps)] for r in range(2)]

    def force_pair(x, it):
        field = field_pair(x) if it else None
        parts = [None] * (2 * comps)
        for r in range(2):
            differ = d0_ref[x + r]
            grads = [gn_ref[c, x + r] for c in range(comps)]
            denom = 1.0
            for c in range(comps):
                denom = denom + grads[c] * grads[c]
                if it:
                    differ = differ + field[r][c] * gm_ref[c, x + r]
            gain = STEP_SIZE * (differ / (denom + differ * differ))
            for c in range(comps):
                pushed_c = gain * grads[c]
                if it:
                    pushed_c = pushed_c + field[r][c]
                high = pushed_c.astype(jnp.bfloat16)
                low = (pushed_c - high.astype(jnp.float32)).astype(jnp.bfloat16)
                parts[2 * c + r] = jnp.concatenate([high, low], axis=1)
        lhs = jnp.concatenate(parts, axis=0)
        out = jnp.dot(lhs, wz_ref[...], preferred_element_type=jnp.float32) * UNSCALE
        for c in range(comps):
            for r in range(2):
                at = (2 * c + r) * width_y
                zs[c, R + x + r] = out[at : at + width_y]

    half = R // 2
    pairs = width_x // 2
    blocks_x, blocks_y = width_x // R, width_y // R
    for it in range(ITERS):

        @pl.loop(0, 2 * half)
        def _(p):
            force_pair(2 * (p + (p // half) * (pairs - 2 * half)), it)

        for c in range(comps):
            for side in (0, 1):
                at = R if side == 0 else width_x
                xsend[it, side, c] = zs[c, at : at + R].astype(jnp.bfloat16)
                start("bx", it, side, c)

        @pl.loop(half, pairs - half)
        def _(p):
            force_pair(2 * p, it)

        for c in range(comps):
            for side in (0, 1):
                at = 0 if side == 0 else R + width_x

                @pl.when(has["bx"][side])
                def _():
                    copy("bx", it, 1 - side, c).wait_recv()
                    zs[c, at : at + R] = xrecv[it, side, c].astype(jnp.float32)

            @pl.loop(0, blocks_x * blocks_y)
            def _(t):
                x0 = (t // blocks_y) * R
                y0 = pl.multiple_of((t % blocks_y) * R, R)
                block = zs[c, pl.ds(x0, 3 * R), pl.ds(y0, R), :]
                total = block[R : 2 * R] * float(EXACT[R])
                for d in range(1, R + 1):
                    total = total + (block[R - d : 2 * R - d] + block[R + d : 2 * R + d]) * float(EXACT[R + d])
                xs[c, pl.ds(x0, R), pl.ds(pl.multiple_of(y0 + R, R), R), :] = total

            @pl.loop(0, blocks_x)
            def _(t):
                for side in (0, 1):
                    at = R if side == 0 else width_y
                    edge = xs[c, pl.ds(t * R, R), at : at + R, :]
                    ysend[it, side, c, pl.ds(t * half, half)] = edge.reshape(half, 2 * R, depth).astype(jnp.bfloat16)

            for side in (0, 1):
                start("by", it, side, c)

        for c in range(comps):
            for side in (0, 1):
                at = 0 if side == 0 else R + width_y

                @pl.when(has["by"][side])
                def _():
                    copy("by", it, 1 - side, c).wait_recv()

                    @pl.loop(0, blocks_x)
                    def _(t):
                        got = yrecv[it, side, c, pl.ds(t * half, half)].astype(jnp.float32)
                        xs[c, pl.ds(t * R, R), at : at + R, :] = got.reshape(R, R, depth)

    @pl.loop(0, pairs)
    def _(p):
        field = field_pair(2 * p)
        for r in range(2):
            for c in range(comps):
                u_ref[c, 2 * p + r] = field[r][c]

    slab = width_x // ny

    def halves_of(x):
        high = x.astype(jnp.bfloat16)
        return high, (x - high.astype(jnp.float32)).astype(jnp.bfloat16)

    def turn(d):
        first_row = order[d] * slab

        @pl.loop(0, slab // 2)
        def _(p):
            x = first_row + 2 * p
            rows = jnp.concatenate([u_ref[c, x + r] for c in range(comps) for r in range(2)], axis=1)
            mid = jnp.dot(sy_ref[...], jnp.concatenate(halves_of(rows), axis=0), preferred_element_type=jnp.float32)
            parts = []
            for k in range(2 * comps):
                parts.append(jnp.concatenate(halves_of(mid[:, k * depth : (k + 1) * depth]), axis=1))
            out = jnp.dot(jnp.concatenate(parts, axis=0), sz_ref[...], preferred_element_type=jnp.float32)
            for c in range(comps):
                for r in range(2):
                    at = (2 * c + r) * width_y
                    tsend[d, c, 2 * p + r] = out[at : at + width_y].astype(jnp.bfloat16)

    def slab_copy(j):
        d = lax.rem(iy + j, ny)
        return pltpu.make_async_remote_copy(
            src_ref=tsend.at[d],
            dst_ref=back_ref.at[iy],
            send_sem=tss.at[j],
            recv_sem=trs.at[j],
            device_id={"by": d},
            device_id_type=pl.DeviceIdType.MESH,
        )

    @pl.loop(1, ny)
    def _(j):
        turn(lax.rem(iy + j, ny))
        slab_copy(j).start()

    turn(iy)
    own = pltpu.make_async_copy(tsend.at[iy], back_ref.at[iy], own_sem)
    own.start()
    own.wait()

    @pl.loop(1, ny)
    def _(j):
        slab_copy(j).wait()

    for n, axis in enumerate(("bx", "by")):
        for side in (0, 1):

            @pl.when(has[axis][side])
            def _():
                edge_copy(n, axis, side).wait_send()

    for it in range(ITERS):
        for axis in ("bx", "by"):
            for side in (0, 1):
                for c in range(comps):

                    @pl.when(has[axis][side])
                    def _():
                        copy(axis, it, side, c).wait_send()


def demons(order, fixed, warped, stretch_y, stretch_z):
    comps = 3
    width_x, width_y, depth = fixed.shape
    grid_x, grid_y = lax.axis_size("bx"), lax.axis_size("by")
    wz = band(depth, depth)
    sy = stretch_y.T.astype(jnp.bfloat16)
    sz = stretch_z.astype(jnp.bfloat16)
    full = pltpu.VMEM((comps, width_x, width_y, depth), jnp.float32)
    slabs = (grid_y, comps, width_x // grid_y, width_y, depth)
    edge_1 = pltpu.VMEM((2, 2, width_y, depth), jnp.bfloat16)
    edge_2 = pltpu.VMEM((2, 2, width_x, depth), jnp.float32)
    vmem = pl.BlockSpec(memory_space=pltpu.VMEM)
    edge_x = pltpu.VMEM((ITERS, 2, comps, RADIUS, width_y, depth), jnp.bfloat16)
    edge_y = pltpu.VMEM((ITERS, 2, comps, width_x // 2, 2 * RADIUS, depth), jnp.bfloat16)
    sems = pltpu.SemaphoreType.DMA((ITERS, 2, comps))
    return pl.pallas_call(
        functools.partial(demons_kernel, grid_x, grid_y),
        out_shape=(
            jax.ShapeDtypeStruct((comps, width_x, width_y, depth), jnp.float32),
            jax.ShapeDtypeStruct(slabs, jnp.bfloat16),
        ),
        in_specs=[pl.BlockSpec(memory_space=pltpu.SMEM)] + [vmem] * 6,
        out_specs=(vmem, pl.BlockSpec(memory_space=pl.ANY)),
        scratch_shapes=[
            pltpu.VMEM((width_x, width_y, depth), jnp.float32),
            full,
            full,
            pltpu.VMEM(slabs, jnp.bfloat16),
            edge_1,
            edge_1,
            edge_2,
            edge_2,
            pltpu.SemaphoreType.DMA((2, 2)),
            pltpu.SemaphoreType.DMA((2, 2)),
            pltpu.SemaphoreType.DMA((grid_y,)),
            pltpu.SemaphoreType.DMA((grid_y,)),
            pltpu.SemaphoreType.DMA,
            pltpu.VMEM((comps, width_x + 2 * RADIUS, width_y, depth), jnp.float32),
            pltpu.VMEM((comps, width_x, width_y + 2 * RADIUS, depth), jnp.float32),
            edge_x,
            edge_x,
            edge_y,
            edge_y,
            sems,
            sems,
            sems,
            sems,
        ],
        compiler_params=pltpu.CompilerParams(collective_id=0, has_side_effects=True, vmem_limit_bytes=62 << 20),
    )(
        order,
        fixed,
        warped,
        band(width_y, width_y + 2 * RADIUS),
        jnp.concatenate([wz, wz], axis=0),
        jnp.concatenate([sy, sy], axis=1),
        jnp.concatenate([sz, sz], axis=0),
    )


def local(fixed_image, moving_image, source_list, stretch_offsets):
    width_x, width_y, depth = fixed_image.shape
    peers = lax.axis_size("by")
    mine = lax.axis_index("by")
    rows_slab = width_x // peers
    lists = source_list[0]
    own_list = lax.dynamic_index_in_dim(lists, mine, 0, keepdims=False)
    slab_ids = jnp.arange(peers)
    asked = (lists == mine).astype(jnp.int32)
    wanted = jnp.sum(asked * slab_ids[None, :], axis=1)
    slabs = moving_image.reshape(peers, rows_slab, width_y, depth)
    outgoing = jnp.take(slabs, wanted, axis=0)
    incoming = lax.all_to_all(outgoing, "by", split_axis=0, concat_axis=0, tiled=True)
    offsets = stretch_offsets[0, 0]
    stretch_y = stretch_matrix(width_y, offsets[0])
    stretch_z = stretch_matrix(depth, offsets[1])
    first = jnp.einsum(
        "yc,pxcz->pxyz",
        stretch_y.astype(jnp.bfloat16),
        incoming,
        preferred_element_type=jnp.float32,
    )
    second = dot_split("pxyz,wz->pxyw", first, stretch_z.astype(jnp.bfloat16))
    stretched = second.astype(jnp.bfloat16)
    warped = jnp.take(stretched, own_list, axis=0).reshape(width_x, width_y, depth)
    inverse = jnp.sum(
        (own_list[None, :] == slab_ids[:, None]).astype(jnp.int32) * slab_ids[None, :], axis=1
    )
    field_u, arriving = demons(inverse.astype(jnp.int32), fixed_image, warped, stretch_y, stretch_z)
    table = asked.astype(jnp.bfloat16)
    back = jnp.einsum("tk,tcxyz->ckxyz", table, arriving, preferred_element_type=jnp.float32)
    back_force = back.reshape(3, width_x, width_y, depth)
    return (field_u, back_force)


def solution(mesh):
    return jax.shard_map(
        local,
        mesh=mesh,
        in_specs=(
            P("bx", "by", None),
            P("bx", "by", None),
            P("bx", None, None),
            P("bx", "by", None),
        ),
        out_specs=(P(None, "bx", "by", None), P(None, "bx", "by", None)),
        check_vma=False,
    )
```

```python
import functools

import jax
import jax.numpy as jnp
import ml_dtypes
import numpy as np
from jax import lax
from jax.experimental import pallas as pl
from jax.experimental.pallas import tpu as pltpu
from jax.sharding import PartitionSpec as P

RADIUS = 8
ITERS = 3


STEP_SIZE = 128.0


def stretch_matrix(length, offset):
    index = jnp.arange(length).astype(jnp.float32)
    place = index + offset.astype(jnp.float32) * (2.0 * index + 1.0 - length) / (2.0 * length)
    place = jnp.clip(place, 0.0, length - 1.0)
    return jnp.maximum(0.0, 1.0 - jnp.abs(place[:, None] - index[None, :]))


def tap_weights():
    spread = 0.75 * RADIUS
    offs = np.arange(-RADIUS, RADIUS + 1).astype(np.float64)
    raw = np.exp(-offs * offs / (2.0 * spread * spread))
    raw = raw / raw.sum()
    best = None
    for scale in np.linspace(4.0, 8.0, 2001):
        near = (raw * scale).astype(ml_dtypes.bfloat16).astype(np.float64)
        err = np.sum((near / near.sum() - raw) ** 2)
        if best is None or err < best[0]:
            best = (err, near)
    near = best[1]
    return raw, near, 1.0 / near.sum()


EXACT, TAPS, UNSCALE = tap_weights()
UNSCALE = float(UNSCALE)


def band(rows, cols):
    start = (cols - rows) // 2
    dist = np.arange(cols)[None, :] - np.arange(rows)[:, None] - start
    inside = np.abs(dist) <= RADIUS
    return jnp.asarray(np.where(inside, TAPS[np.clip(dist + RADIUS, 0, 2 * RADIUS)], 0.0).astype(ml_dtypes.bfloat16))


def dot(spec, a, b):
    return jnp.einsum(spec, a, b, preferred_element_type=jnp.float32)


def halves(x):
    high = lax.reduce_precision(x, 8, 7)
    return high.astype(jnp.bfloat16), (x - high).astype(jnp.bfloat16)


def dot_split(spec, x, w):
    high, low = halves(x)
    return dot(spec, high, w) + dot(spec, low, w)


def unrolled(start, stop, most=4):
    size = max(u for u in (1, 2, 4) if u <= most and (stop - start) % u == 0)

    def wrap(body):
        @pl.loop(0, (stop - start) // size)
        def _(t):
            for r in range(size):
                body(start + t * size + r)

    return wrap


def demons_kernel(nx, ny, order, fixed_ref, warped_ref, wy_ref, wz_ref, sy_ref, sz_ref, u_ref, back_ref, d0_ref, gm_ref, gn_ref, tsend, esx, erx, esy, ery, ess, ers, tss, trs, own_sem, zs, xs, xsend, xrecv, ysend, yrecv, xss, xrs, yss, yrs):
    comps, width_x, width_y, depth = gm_ref.shape
    ix, iy = lax.axis_index("bx"), lax.axis_index("by")
    has = {"bx": (ix > 0, ix < nx - 1), "by": (iy > 0, iy < ny - 1)}
    dev = {
        "bx": (lax.rem(ix + nx - 1, nx), lax.rem(ix + 1, nx)),
        "by": (lax.rem(iy + ny - 1, ny), lax.rem(iy + 1, ny)),
    }
    barrier = pltpu.get_barrier_semaphore()
    for side in (0, 1):

        @pl.when(has["bx"][side])
        def _():
            pl.semaphore_signal(barrier, inc=1, device_id={"bx": dev["bx"][side]}, device_id_type=pl.DeviceIdType.MESH)

    for j in range(1, ny):
        pl.semaphore_signal(barrier, inc=1, device_id={"by": lax.rem(iy + j, ny)}, device_id_type=pl.DeviceIdType.MESH)
    met = sum(ok.astype(jnp.int32) for ok in has["bx"]) + (ny - 1)
    pl.semaphore_wait(barrier, met)

    R = RADIUS

    def edge_copy(n, axis, side):
        send, recv = (esx, erx) if axis == "bx" else (esy, ery)
        return pltpu.make_async_remote_copy(
            src_ref=send.at[side],
            dst_ref=recv.at[1 - side],
            send_sem=ess.at[n, side],
            recv_sem=ers.at[n, 1 - side],
            device_id={axis: dev[axis][side]},
            device_id_type=pl.DeviceIdType.MESH,
        )

    images = (fixed_ref, warped_ref)
    for m in range(2):
        esx[0, m] = images[m][0]
        esx[1, m] = images[m][width_x - 1]

    @pl.loop(0, width_x)
    def _(x):
        for m in range(2):
            row = images[m][x].astype(jnp.float32)
            zs[m, R + x] = row
            esy[0, m, pl.ds(x, 1), :] = row[0:1]
            esy[1, m, pl.ds(x, 1), :] = row[width_y - 1 : width_y]

    for n, axis in enumerate(("bx", "by")):
        for side in (0, 1):

            @pl.when(has[axis][side])
            def _():
                edge_copy(n, axis, side).start()

    for side in (0, 1):
        at = R - 1 if side == 0 else R + width_x

        @pl.when(has["bx"][side])
        def _():
            edge_copy(0, "bx", 1 - side).wait_recv()
            for m in range(2):
                zs[m, at] = erx[side, m].astype(jnp.float32)

        @pl.when(jnp.logical_not(has["bx"][side]))
        def _():
            for m in range(2):
                zs[m, at] = jnp.zeros((width_y, depth), jnp.float32)

        @pl.when(has["by"][side])
        def _():
            edge_copy(1, "by", 1 - side).wait_recv()

        @pl.when(jnp.logical_not(has["by"][side]))
        def _():
            ery[side] = jnp.zeros(ery.shape[1:], jnp.float32)

    at_y = lax.broadcasted_iota(jnp.int32, (width_y, depth), 0)
    at_z = lax.broadcasted_iota(jnp.int32, (width_y, depth), 1)

    @unrolled(0, width_x, 2)
    def _(x):
        both = []
        for m in range(2):
            row = zs[m, R + x]
            grad_x = (zs[m, R + x + 1] - zs[m, R + x - 1]) * 0.5
            low = jnp.where(at_y == 0, ery[0, m, pl.ds(x, 1), :], pltpu.roll(row, 1, 0))
            high = jnp.where(at_y == width_y - 1, ery[1, m, pl.ds(x, 1), :], pltpu.roll(row, width_y - 1, 0))
            grad_y = (high - low) * 0.5
            low = jnp.where(at_z == 0, 0.0, pltpu.roll(row, 1, 1))
            high = jnp.where(at_z == depth - 1, 0.0, pltpu.roll(row, depth - 1, 1))
            both.append((grad_x, grad_y, (high - low) * 0.5))
        for c in range(comps):
            gm_ref[c, x] = both[1][c]
            gn_ref[c, x] = 0.5 * (both[0][c] + both[1][c])
        d0_ref[x] = zs[1, R + x] - zs[0, R + x]

    def copy(axis, it, side, c):
        send, recv, ss, rs = (xsend, xrecv, xss, xrs) if axis == "bx" else (ysend, yrecv, yss, yrs)
        return pltpu.make_async_remote_copy(
            src_ref=send.at[it, side, c],
            dst_ref=recv.at[it, 1 - side, c],
            send_sem=ss.at[it, side, c],
            recv_sem=rs.at[it, 1 - side, c],
            device_id={axis: dev[axis][side]},
            device_id_type=pl.DeviceIdType.MESH,
        )

    def start(axis, it, side, c):
        @pl.when(has[axis][side])
        def _():
            copy(axis, it, side, c).start()

    for side in (0, 1):
        at_x = 0 if side == 0 else R + width_x
        at_y = 0 if side == 0 else R + width_y

        @pl.when(jnp.logical_not(has["bx"][side]))
        def _():
            for c in range(comps):
                zs[c, at_x : at_x + R] = jnp.zeros((R, width_y, depth), jnp.float32)

        @pl.when(jnp.logical_not(has["by"][side]))
        def _():
            for c in range(comps):
                xs[c, :, at_y : at_y + R, :] = jnp.zeros((width_x, R, depth), jnp.float32)

    def field_pair(x):
        rhs = jnp.concatenate([xs[c, x + r] for c in range(comps) for r in range(2)], axis=1).astype(jnp.bfloat16)
        out = jnp.dot(wy_ref[...], rhs, preferred_element_type=jnp.float32) * UNSCALE
        return [[out[:, (2 * c + r) * depth : (2 * c + r + 1) * depth] for c in range(comps)] for r in range(2)]

    def force_pair(x, it):
        field = field_pair(x) if it else None
        parts = [None] * (2 * comps)
        for r in range(2):
            differ = d0_ref[x + r]
            grads = [gn_ref[c, x + r] for c in range(comps)]
            denom = 1.0
            for c in range(comps):
                denom = denom + grads[c] * grads[c]
                if it:
                    differ = differ + field[r][c] * gm_ref[c, x + r]
            gain = STEP_SIZE * (differ / (denom + differ * differ))
            for c in range(comps):
                pushed_c = gain * grads[c]
                if it:
                    pushed_c = pushed_c + field[r][c]
                high = pushed_c.astype(jnp.bfloat16)
                low = (pushed_c - high.astype(jnp.float32)).astype(jnp.bfloat16)
                parts[2 * c + r] = jnp.concatenate([high, low], axis=1)
        lhs = jnp.concatenate(parts, axis=0)
        out = jnp.dot(lhs, wz_ref[...], preferred_element_type=jnp.float32) * UNSCALE
        for c in range(comps):
            for r in range(2):
                at = (2 * c + r) * width_y
                zs[c, R + x + r] = out[at : at + width_y]

    half = R // 2
    pairs = width_x // 2
    blocks_x, blocks_y = width_x // R, width_y // R
    for it in range(ITERS):

        @unrolled(0, 2 * half)
        def _(p):
            force_pair(2 * (p + (p // half) * (pairs - 2 * half)), it)

        for c in range(comps):
            for side in (0, 1):
                at = R if side == 0 else width_x
                xsend[it, side, c] = zs[c, at : at + R].astype(jnp.bfloat16)
                start("bx", it, side, c)

        @unrolled(half, pairs - half)
        def _(p):
            force_pair(2 * p, it)

        for c in range(comps):
            for side in (0, 1):
                at = 0 if side == 0 else R + width_x

                @pl.when(has["bx"][side])
                def _():
                    copy("bx", it, 1 - side, c).wait_recv()
                    zs[c, at : at + R] = xrecv[it, side, c].astype(jnp.float32)

            @unrolled(0, blocks_x * blocks_y)
            def _(t):
                x0 = (t // blocks_y) * R
                y0 = pl.multiple_of((t % blocks_y) * R, R)
                block = zs[c, pl.ds(x0, 3 * R), pl.ds(y0, R), :]
                total = block[R : 2 * R] * float(EXACT[R])
                for d in range(1, R + 1):
                    total = total + (block[R - d : 2 * R - d] + block[R + d : 2 * R + d]) * float(EXACT[R + d])
                xs[c, pl.ds(x0, R), pl.ds(pl.multiple_of(y0 + R, R), R), :] = total

            @pl.loop(0, blocks_x)
            def _(t):
                for side in (0, 1):
                    at = R if side == 0 else width_y
                    edge = xs[c, pl.ds(t * R, R), at : at + R, :]
                    ysend[it, side, c, pl.ds(t * half, half)] = edge.reshape(half, 2 * R, depth).astype(jnp.bfloat16)

            for side in (0, 1):
                start("by", it, side, c)

        for c in range(comps):
            for side in (0, 1):
                at = 0 if side == 0 else R + width_y

                @pl.when(has["by"][side])
                def _():
                    copy("by", it, 1 - side, c).wait_recv()

                    @pl.loop(0, blocks_x)
                    def _(t):
                        got = yrecv[it, side, c, pl.ds(t * half, half)].astype(jnp.float32)
                        xs[c, pl.ds(t * R, R), at : at + R, :] = got.reshape(R, R, depth)

    @unrolled(0, pairs)
    def _(p):
        field = field_pair(2 * p)
        for r in range(2):
            for c in range(comps):
                u_ref[c, 2 * p + r] = field[r][c]

    slab = width_x // ny

    def halves_of(x):
        high = x.astype(jnp.bfloat16)
        return high, (x - high.astype(jnp.float32)).astype(jnp.bfloat16)

    def turn(d):
        first_row = order[d] * slab

        @unrolled(0, slab // 2)
        def _(p):
            x = first_row + 2 * p
            rows = jnp.concatenate([u_ref[c, x + r] for c in range(comps) for r in range(2)], axis=1)
            mid = jnp.dot(sy_ref[...], jnp.concatenate(halves_of(rows), axis=0), preferred_element_type=jnp.float32)
            parts = []
            for k in range(2 * comps):
                parts.append(jnp.concatenate(halves_of(mid[:, k * depth : (k + 1) * depth]), axis=1))
            out = jnp.dot(jnp.concatenate(parts, axis=0), sz_ref[...], preferred_element_type=jnp.float32)
            for c in range(comps):
                for r in range(2):
                    at = (2 * c + r) * width_y
                    tsend[d, c, 2 * p + r] = out[at : at + width_y].astype(jnp.bfloat16)

    def slab_copy(j):
        d = lax.rem(iy + j, ny)
        return pltpu.make_async_remote_copy(
            src_ref=tsend.at[d],
            dst_ref=back_ref.at[iy],
            send_sem=tss.at[j],
            recv_sem=trs.at[j],
            device_id={"by": d},
            device_id_type=pl.DeviceIdType.MESH,
        )

    @pl.loop(1, ny)
    def _(j):
        turn(lax.rem(iy + j, ny))
        slab_copy(j).start()

    turn(iy)
    own = pltpu.make_async_copy(tsend.at[iy], back_ref.at[iy], own_sem)
    own.start()
    own.wait()

    @pl.loop(1, ny)
    def _(j):
        slab_copy(j).wait()

    for n, axis in enumerate(("bx", "by")):
        for side in (0, 1):

            @pl.when(has[axis][side])
            def _():
                edge_copy(n, axis, side).wait_send()

    for it in range(ITERS):
        for axis in ("bx", "by"):
            for side in (0, 1):
                for c in range(comps):

                    @pl.when(has[axis][side])
                    def _():
                        copy(axis, it, side, c).wait_send()


def demons(order, fixed, warped, stretch_y, stretch_z):
    comps = 3
    width_x, width_y, depth = fixed.shape
    grid_x, grid_y = lax.axis_size("bx"), lax.axis_size("by")
    wz = band(depth, depth)
    sy = stretch_y.T.astype(jnp.bfloat16)
    sz = stretch_z.astype(jnp.bfloat16)
    full = pltpu.VMEM((comps, width_x, width_y, depth), jnp.float32)
    slabs = (grid_y, comps, width_x // grid_y, width_y, depth)
    edge_1 = pltpu.VMEM((2, 2, width_y, depth), jnp.bfloat16)
    edge_2 = pltpu.VMEM((2, 2, width_x, depth), jnp.float32)
    vmem = pl.BlockSpec(memory_space=pltpu.VMEM)
    edge_x = pltpu.VMEM((ITERS, 2, comps, RADIUS, width_y, depth), jnp.bfloat16)
    edge_y = pltpu.VMEM((ITERS, 2, comps, width_x // 2, 2 * RADIUS, depth), jnp.bfloat16)
    sems = pltpu.SemaphoreType.DMA((ITERS, 2, comps))
    return pl.pallas_call(
        functools.partial(demons_kernel, grid_x, grid_y),
        out_shape=(
            jax.ShapeDtypeStruct((comps, width_x, width_y, depth), jnp.float32),
            jax.ShapeDtypeStruct(slabs, jnp.bfloat16),
        ),
        in_specs=[pl.BlockSpec(memory_space=pltpu.SMEM)] + [vmem] * 6,
        out_specs=(vmem, pl.BlockSpec(memory_space=pl.ANY)),
        scratch_shapes=[
            pltpu.VMEM((width_x, width_y, depth), jnp.float32),
            full,
            full,
            pltpu.VMEM(slabs, jnp.bfloat16),
            edge_1,
            edge_1,
            edge_2,
            edge_2,
            pltpu.SemaphoreType.DMA((2, 2)),
            pltpu.SemaphoreType.DMA((2, 2)),
            pltpu.SemaphoreType.DMA((grid_y,)),
            pltpu.SemaphoreType.DMA((grid_y,)),
            pltpu.SemaphoreType.DMA,
            pltpu.VMEM((comps, width_x + 2 * RADIUS, width_y, depth), jnp.float32),
            pltpu.VMEM((comps, width_x, width_y + 2 * RADIUS, depth), jnp.float32),
            edge_x,
            edge_x,
            edge_y,
            edge_y,
            sems,
            sems,
            sems,
            sems,
        ],
        compiler_params=pltpu.CompilerParams(collective_id=0, has_side_effects=True, vmem_limit_bytes=62 << 20),
    )(
        order,
        fixed,
        warped,
        band(width_y, width_y + 2 * RADIUS),
        jnp.concatenate([wz, wz], axis=0),
        jnp.concatenate([sy, sy], axis=1),
        jnp.concatenate([sz, sz], axis=0),
    )


def sum_kernel(wanted, slabs_ref, out_ref):
    out_ref[...] = jnp.zeros(out_ref.shape, jnp.float32)
    for t in range(slabs_ref.shape[0]):

        @pl.when(wanted[t] == pl.program_id(0))
        def _():
            out_ref[...] += slabs_ref[t].astype(jnp.float32)


def slab_sums(wanted, slabs):
    peers, comps, rows, width_y, depth = slabs.shape
    return pl.pallas_call(
        sum_kernel,
        out_shape=jax.ShapeDtypeStruct((comps, peers * rows, width_y, depth), jnp.float32),
        grid_spec=pltpu.PrefetchScalarGridSpec(
            num_scalar_prefetch=1,
            grid=(peers,),
            in_specs=[pl.BlockSpec(slabs.shape, lambda k, ids: (0, 0, 0, 0, 0), pipeline_mode=pl.Buffered(1))],
            out_specs=pl.BlockSpec((comps, rows, width_y, depth), lambda k, ids: (0, k, 0, 0)),
        ),
    )(wanted, slabs)


def local(fixed_image, moving_image, source_list, stretch_offsets):
    width_x, width_y, depth = fixed_image.shape
    peers = lax.axis_size("by")
    mine = lax.axis_index("by")
    rows_slab = width_x // peers
    lists = source_list[0]
    own_list = lax.dynamic_index_in_dim(lists, mine, 0, keepdims=False)
    slab_ids = jnp.arange(peers)
    asked = (lists == mine).astype(jnp.int32)
    wanted = jnp.sum(asked * slab_ids[None, :], axis=1)
    slabs = moving_image.reshape(peers, rows_slab, width_y, depth)
    outgoing = jnp.take(slabs, wanted, axis=0)
    incoming = lax.all_to_all(outgoing, "by", split_axis=0, concat_axis=0, tiled=True)
    offsets = stretch_offsets[0, 0]
    stretch_y = stretch_matrix(width_y, offsets[0])
    stretch_z = stretch_matrix(depth, offsets[1])
    first = jnp.einsum(
        "yc,pxcz->pxyz",
        stretch_y.astype(jnp.bfloat16),
        incoming,
        preferred_element_type=jnp.float32,
    )
    second = dot_split("pxyz,wz->pxyw", first, stretch_z.astype(jnp.bfloat16))
    stretched = second.astype(jnp.bfloat16)
    warped = jnp.take(stretched, own_list, axis=0).reshape(width_x, width_y, depth)
    inverse = jnp.sum(
        (own_list[None, :] == slab_ids[:, None]).astype(jnp.int32) * slab_ids[None, :], axis=1
    )
    field_u, arriving = demons(inverse.astype(jnp.int32), fixed_image, warped, stretch_y, stretch_z)
    back_force = slab_sums(wanted.astype(jnp.int32), arriving)
    return (field_u, back_force)


def solution(mesh):
    return jax.shard_map(
        local,
        mesh=mesh,
        in_specs=(
            P("bx", "by", None),
            P("bx", "by", None),
            P("bx", None, None),
            P("bx", "by", None),
        ),
        out_specs=(P(None, "bx", "by", None), P(None, "bx", "by", None)),
        check_vma=False,
    )
```
